32 devices in a mesh: group: 2 (over y), gz: 4 (over z), gy: 2 (over x), gx: 2 (over core).
Axes of the slice: x: 2, y: 2, z: 4, core: 2. Of those that a mesh axis runs over, the one named last changes fastest.
Arguments:
- volume: bfloat16 [32, 32, 16, 512], P(None, ('group', 'gz'), 'gy', 'gx'), parts along dimension 1, may hold values from -6 to 6
- first_weight: bfloat16 [3, 3, 3, 32, 32], replicated, may hold values from -0.21875 to 0.21875
- second_weight: bfloat16 [3, 3, 3, 32, 32], replicated, may hold values from -0.21875 to 0.21875
- sample_index: int32 [8, 2, 2, 256], P(('group', 'gz'), 'gy', 'gx'), parts along dimension 0, may hold values from 0 to 8191
- segments: int32 [8, 2, 2, 256], P('group', 'gy', 'gx'), parts along dimension 0, may hold values from 0 to 63
- block_match: int32 [8, 4], P('group'), parts along dimension 0, may hold values from 0 to 1, as said below
Outputs:
- features: bfloat16 [32, 32, 16, 512], P(None, ('group', 'gz'), 'gy', 'gx'), parts along dimension 1
- row_loss: float32 [8, 2, 2, 256], P(('group', 'gz'), 'gy', 'gx'), parts along dimension 0
The draws below stay inside these ranges and needn't reach their ends.
There are 2 independent parts, one for each index of `group`. The reference program is written for one: setup_inputs(seed, part) draws one part's arguments, and reference() takes and returns one part's arrays. A program takes and returns all parts, laid end to end along the dimension named above; an argument that names none is the same for every part. Nothing has to cross between parts.
Inputs may be any that keep to these rules, and one draw needn't show every extreme that they name: `sample_index`: the voxel of a row is z * 8 * 256 + y * 256 + x in its block's local coordinates. `block_match`: entry [a, a2] is 1 when block a contrasts against block a2; the diagonal is 1.
All inputs are finite; a program needn't handle non-finite values.
Results may differ from the reference program's by a relative error of at most 0.0034.
Values may be sent and summed in bfloat16 or wider, within the bound.
A program may use at most 128 MiB of HBM per device.

```python
import jax
import jax.numpy as jnp
from jax import lax

C = 32
CZ = 4
CY = 8
CX = 256
R = 256
NSEG = 64
NZB = 4
NZ = 16
NY = 16
NX = 512
N_GY = 2
N_GX = 2


def draw_block_match(key, part):
    random_bits = jax.random.randint(key, (NZB, NZB), 0, 2)
    diagonal = (jnp.arange(NZB)[:, None] == jnp.arange(NZB)[None, :]).astype(jnp.int32)
    return jnp.maximum(random_bits, diagonal).astype(jnp.int32)


def plant(entries, rng, least, high):
    index_at = [jax.random.randint(jax.random.fold_in(rng, axis), (), 0, length) for axis, length in enumerate(entries.shape)]
    main_axis = entries.shape.index(max(entries.shape))
    next_to = index_at[:main_axis] + [(index_at[main_axis] + 1) % entries.shape[main_axis]] + index_at[main_axis + 1:]
    return entries.at[tuple(index_at)].set(least).at[tuple(next_to)].set(high)


def level_of(key, extent, split, least, high):
    gain = 1.0
    for position, shards_of in split:
        heights = jax.random.uniform(jax.random.fold_in(jax.random.fold_in(key, 6), position), (shards_of,), jnp.float32, least / len(split), high / len(split))
        gain = gain * jnp.repeat(jnp.exp(heights), extent[position] // shards_of).reshape((-1,) + (1,) * (len(extent) - 1 - position))
    return gain


def bell_draw(key, dims, deviation, bound, cuts=(), kind=jnp.bfloat16):
    result = deviation * jax.random.normal(key, dims, jnp.float32)
    if cuts:
        result = result * level_of(key, dims, cuts, -0.22, 0.18)
    return jnp.clip(result, -bound, bound).astype(kind)


def setup_inputs(seed: int = 0, part: int = 0) -> dict:
    splits = jax.random.split(jax.random.key(seed), 7)
    part_keys = jax.random.split(jax.random.fold_in(splits[6], part), 7)
    volume = bell_draw(part_keys[0], (C, NZ, NY, NX), 1.0, 6.0, ((1, 4), (2, 2), (3, 2)))
    first_weight = bell_draw(splits[1], (3, 3, 3, C, C), (27 * C) ** -0.5, 0.21875)
    second_weight = bell_draw(splits[2], (3, 3, 3, C, C), (27 * C) ** -0.5, 0.21875)
    sample_index = plant(jax.random.randint(part_keys[3], (NZB, N_GY, N_GX, R), 0, CZ * CY * CX), jax.random.fold_in(part_keys[3], 1), 0, (CZ * CY * CX) - 1).astype(jnp.int32)
    segments = plant(jax.random.randint(part_keys[4], (NZB, N_GY, N_GX, R), 0, NSEG), jax.random.fold_in(part_keys[4], 1), 0, NSEG - 1).astype(jnp.int32)
    block_match = draw_block_match(jax.random.fold_in(jax.random.fold_in(splits[6], part), 71), part)
    return {"volume": volume, "first_weight": first_weight, "second_weight": second_weight, "sample_index": sample_index, "segments": segments, "block_match": block_match}


SOFTMAX_WARMTH = 0.25

def conv_same(activ_in, weight):
    padded = jnp.pad(activ_in.astype(jnp.float32), ((0, 0), (1, 1), (1, 1), (1, 1)))
    kernel = weight.astype(jnp.float32)
    out_y = activ_in.shape[2]
    out_x = activ_in.shape[3]

    def slab(block_id):
        window = lax.dynamic_slice_in_dim(padded, (block_id * CZ).astype(jnp.int32), CZ + 2, 1)
        reduced_total = jnp.zeros((kernel.shape[3], CZ, out_y, out_x), jnp.float32)
        for offset_z in range(3):
            for offset_y in range(3):
                for column_shift in range(3):
                    reduced_total = reduced_total + jnp.einsum('oi,izyx->ozyx', kernel[offset_z, offset_y, column_shift], window[:, offset_z:offset_z + CZ, offset_y:offset_y + out_y, column_shift:column_shift + out_x])
        return reduced_total
    slabs = lax.map(slab, jnp.arange(NZB, dtype=jnp.int32))
    return jnp.moveaxis(slabs, 0, 1).reshape(kernel.shape[3], NZB * CZ, out_y, out_x)

def reference(volume, first_weight, second_weight, sample_index, segments, block_match):
    hidden = jax.nn.relu(conv_same(volume, first_weight)).astype(jnp.bfloat16)
    features = (conv_same(hidden, second_weight) + volume.astype(jnp.float32)).astype(jnp.bfloat16)
    local_z = sample_index // (CY * CX)
    local_y = sample_index // CX % CY
    local_x = sample_index % CX
    glob_z = local_z + jnp.arange(NZB, dtype=jnp.int32)[:, None, None, None] * CZ
    global_row_coord = local_y + jnp.arange(N_GY, dtype=jnp.int32)[None, :, None, None] * CY
    glob_x = local_x + jnp.arange(N_GX, dtype=jnp.int32)[None, None, :, None] * CX
    picked = features[:, glob_z, global_row_coord, glob_x].astype(jnp.float32)
    embedding = (picked / jnp.sqrt(lax.optimization_barrier(jnp.sum(picked * picked, axis=0)) + 1.0)).astype(jnp.bfloat16)
    tiles = N_GY * N_GX
    emb_cols = jnp.moveaxis(embedding.reshape(embedding.shape[0], NZB, tiles, R), 2, 0)
    seg_cols = jnp.moveaxis(segments.reshape(NZB, tiles, R), 1, 0)
    weights = block_match.astype(jnp.float32)[:, None, :, None]

    def column(pair):
        emb_col, seg_col = pair
        embedding_flat = emb_col.astype(jnp.float32)
        similarity_logits = jnp.einsum('tru,tdk->rudk', embedding_flat, embedding_flat) / SOFTMAX_WARMTH
        exp_terms = jnp.exp(similarity_logits) * weights
        same_seg = (seg_col[:, :, None, None] == seg_col[None, None, :, :]).astype(jnp.float32)
        reduced_total = lax.optimization_barrier(jnp.sum(exp_terms, axis=(2, 3)))
        positive = lax.optimization_barrier(jnp.sum(exp_terms * same_seg, axis=(2, 3)))
        return jnp.log(reduced_total) - jnp.log(positive)
    losses = lax.map(column, (emb_cols, seg_cols))
    row_loss = jnp.moveaxis(losses, 0, 1).reshape(NZB, N_GY, N_GX, R)
    return (features, row_loss)
```

```python
import functools

import jax
import jax.numpy as jnp
from jax import lax
from jax.experimental import pallas as pl
from jax.experimental.pallas import tpu as pltpu
from jax.sharding import PartitionSpec as P

BF = jnp.bfloat16
F32 = jnp.float32
MESH = pl.DeviceIdType.MESH
HALO = (
    ("near", 1, 0), ("near", -1, 0), ("row", 0, 1), ("row", 0, -1),
    ("near", 1, 1), ("near", 1, -1), ("near", -1, 1), ("near", -1, -1),
    ("far", 1, 0), ("far", -1, 0),
    ("far", 1, 1), ("far", 1, -1), ("far", -1, 1), ("far", -1, -1),
)
SEAM = tuple((core, dz, dy) for dy in (0, 1, -1) for dz in (0, 1, -1) for core in (1, 0) if (core, dz, dy) != (0, 0, 0))
NSEG = 64
OUT1, OUT2 = 160, 128


def iota(shape, dim):
    return lax.broadcasted_iota(jnp.int32, shape, dim)


def mm(a, b):
    return jnp.dot(a, b, preferred_element_type=F32)


def mm_tn(a, b):
    return lax.dot_general(a, b, (((0,), (0,)), ((), ())), preferred_element_type=F32)


def mm_nt(a, b):
    return lax.dot_general(a, b, (((1,), (1,)), ((), ())), preferred_element_type=F32)


def one_hot(mask):
    return jnp.where(mask, 1.0, 0.0).astype(BF)


def kernel(n_gz, n_gy, vol_hbm, w1_hbm, w2_hbm, sidx_hbm, seg_hbm, bm_hbm, feat, loss,
           vol, wts, sidx, seg, bm, v, h, band1, band2, part1, part2, seam, cols, t, hs,
           made, same, emb_all, acc,
           in_sem, send_sem, recv_sem, ss_sem, sr_sem, es_sem, er_sem):
    gz, gy, gx = lax.axis_index("gz"), lax.axis_index("gy"), lax.axis_index("gx")
    other = 1 - gx

    def inside(dz, dy):
        z, y = gz + dz, gy + dy
        return (z >= 0) & (z < n_gz) & (y >= 0) & (y < n_gy)

    def dev(z, y, x):
        return {"gz": z, "gy": y, "gx": x}

    loads = [pltpu.make_async_copy(vol_hbm.at[:, z], vol.at[z], in_sem.at[z]) for z in range(4)]
    more = [
        pltpu.make_async_copy(a, b, in_sem.at[4 + i])
        for i, (a, b) in enumerate((
            (w1_hbm, wts.at[0]), (w2_hbm, wts.at[1]), (sidx_hbm, sidx), (seg_hbm, seg), (bm_hbm, bm)))
    ]
    for z in (0, 3, 1, 2):
        loads[z].start()
    for load in more:
        load.start()

    barrier = pltpu.get_barrier_semaphore()
    count = jnp.int32(n_gz - 1)
    for core, dz, dy in SEAM:
        if core == 1 or dy != 0:
            there = inside(dz, dy)
            count = count + there.astype(jnp.int32)

            @pl.when(there)
            def _():
                pl.semaphore_signal(
                    barrier, inc=1, device_id=dev(gz + dz, gy + dy, other if core else gx), device_id_type=MESH)
    for off in range(1, n_gz):
        pl.semaphore_signal(barrier, inc=1, device_id=dev(lax.rem(gz + off, n_gz), gy, gx), device_id_type=MESH)

    def rows_of(dy):
        if dy == 0:
            return slice(64, 320), slice(64, 320)
        return (slice(256, 320), slice(0, 64)) if dy == 1 else (slice(64, 128), slice(320, 384))

    def planes_of(kind, dz):
        if kind == "row":
            return slice(2, 6), slice(2, 6)
        if kind == "near":
            return (slice(5, 6), slice(1, 2)) if dz == 1 else (slice(2, 3), slice(6, 7))
        return (slice(4, 5), slice(0, 1)) if dz == 1 else (slice(3, 4), slice(7, 8))

    def halo_copy(d):
        kind, dz, dy = HALO[d]
        sr, dr = rows_of(dy)
        sp, dp = planes_of(kind, dz)
        return pltpu.make_async_remote_copy(
            src_ref=v.at[sp, sr, 256:512], dst_ref=v.at[dp, dr, 256:512], send_sem=send_sem.at[d], recv_sem=recv_sem.at[d],
            device_id=dev(gz + dz, gy + dy, gx), device_id_type=MESH)

    def seam_copy(k):
        core, dz, dy = SEAM[k]
        return pltpu.make_async_remote_copy(
            src_ref=seam, dst_ref=cols.at[1 - dy, core, 1 - dz], send_sem=ss_sem.at[k], recv_sem=sr_sem.at[k],
            device_id=dev(gz + dz, gy + dy, other if core else gx), device_id_type=MESH)

    def each(sign, act, *kinds):
        for d, (kind, dz, dy) in enumerate(HALO):
            if (kind if dy == 0 or dz == 0 else kind + "_corner") in kinds:
                @pl.when(inside(sign * dz, sign * dy))
                def _():
                    act(halo_copy(d))

    def each_seam(sign, act):
        for k, (_, dz, dy) in enumerate(SEAM):
            @pl.when(inside(sign * dz, sign * dy))
            def _():
                act(seam_copy(k))

    def start(copy):
        copy.start()

    def wait_recv(copy):
        copy.wait_recv()

    def wait_send(copy):
        copy.wait_send()

    for kind, dz, dy in HALO:
        @pl.when(jnp.logical_not(inside(-dz, -dy)))
        def _():
            rows, planes = rows_of(dy)[1], planes_of(kind, dz)[1]
            v[planes, rows, 256:512] = jnp.zeros((planes.stop - planes.start, rows.stop - rows.start, 256), BF)
    for core, dz, dy in SEAM:
        if (dz, dy) != (0, 0):
            @pl.when(jnp.logical_not(inside(-dz, -dy)))
            def _():
                cols[1 - dy, core, 1 - dz] = jnp.zeros((16, 256), BF)
    v[:, 384:416, :] = jnp.zeros((8, 32, 768), BF)
    h[:, 320:384, :] = jnp.zeros((6, 64, 768), BF)
    t[384:416, :] = jnp.zeros((32, 128), F32)

    rr, cc = iota((256, 256), 0), iota((256, 256), 1)
    edge_lane = 255 * other
    side = 2 * other
    to_yc = one_hot(cc == (rr & 31) * 8 + (rr >> 5))

    def turn(z):
        loads[z].wait()
        v[z + 2, 64:320, 256:512] = mm(to_yc, vol[z].astype(F32).reshape(256, 256).astype(BF)).astype(BF)

    turn(0)
    turn(3)
    pl.semaphore_wait(barrier, count)
    each(1, start, "near")
    turn(1)
    turn(2)
    each(1, start, "row")

    r16, l16 = iota((16, 256), 0), iota((16, 256), 1)
    lane = edge_lane + (r16 >> 2) * (1 - 2 * other)
    packed = jnp.zeros((16, 256), F32)
    for z in range(4):
        mask = (r16 < 8) & ((r16 & 3) == z) & (l16 == lane)
        packed = packed + mm_nt(one_hot(mask), v[z + 2, 64:320, 256:512])
    seam[...] = packed.astype(BF)
    cols[1, 0, 1] = packed.astype(BF)
    each_seam(1, start)
    each(1, start, "near_corner")
    each(1, start, "far")
    each(1, start, "far_corner")

    for load in more:
        load.wait()

    def build(r, band, n_out):
        place = iota((32, 96), 1) - iota((32, 96), 0)
        wide = jnp.zeros((288, 96), F32)
        for b in range(3):
            wide = wide + mm(wts[r, :, b].reshape(288, 32), one_hot(place == 32 * b))
        wide = wide.astype(BF)
        tap, col = iota((96, 256 * n_out), 0), iota((96, 256 * n_out), 1)
        rows = mm(wide, one_hot(tap == (col & 255) - 32 * (col >> 8))).astype(BF)
        for y in range(n_out):
            for n in range(9):
                band[32 * y:32 * y + 32, 256 * n:256 * n + 256] = rows[32 * n:32 * n + 32, 256 * y:256 * y + 256]

    build(0, band1, 5)
    build(1, band2, 4)
    label = iota((NSEG, 256), 0)
    own_seg = one_hot(label == seg[gz])
    for off in range(n_gz):
        block = lax.rem(gz + n_gz - off, n_gz)
        same[off] = mm_tn(one_hot(label == seg[block]), own_seg)

    def window(ref, p, n, first):
        return jnp.concatenate(
            [ref[p + i, first:first + 256, 256 * c:256 * c + 256] for i in range(n) for c in range(3)], axis=0)

    def product(band, ref, p, lo, hi, first):
        return mm(band[:, 768 * lo:768 * hi], window(ref, p + lo, hi - lo, first))

    def widened(x, col):
        lanes = iota(x.shape, 1)
        left = jnp.where(lanes == 0, jnp.where(gx == 1, col, 0.0), pltpu.roll(x, 1, 1))
        right = jnp.where(lanes == 255, jnp.where(gx == 0, col, 0.0), pltpu.roll(x, 255, 1))
        return left.astype(BF), right.astype(BF)

    def widen(p):
        x = v[p, 0:384, 256:512].astype(F32)
        v[p, 0:384, 0:256], v[p, 0:384, 512:768] = widened(x, t[0:384, 8 + p:9 + p])

    def valid(shape, q, first):
        row = iota(shape, 0) + first
        ok = ((row >= 32) | (gy > 0)) & ((row < 288) | (gy < n_gy - 1))
        return ok & ((q > 0) | (gz > 0)) & ((q < 5) | (gz < n_gz - 1))

    def hide(q, g, x):
        at = slice(OUT1 * g, OUT1 * g + OUT1)
        x = jnp.where(valid((OUT1, 256), q, OUT1 * g), jnp.maximum(x, 0.0), 0.0)
        h[q, at, 256:512] = x.astype(BF)
        h[q, at, 0:256], h[q, at, 512:768] = widened(x, hs[at, q:q + 1])

    def seams():
        row, col = iota((96, 128), 0), iota((96, 128), 1)
        core = jnp.where(row >= 48, 1, 0)
        row = row - 48 * core
        j = (row & 15) >> 2
        plane = (row & 3) + 4 * (row >> 4) - 2
        tap = jnp.where(core == 0, 2 - side, jnp.where(j == 0, 1, side))
        put = one_hot((j + (1 - core) < 2) & (plane >= 0) & (plane < 8) & (col == 8 * tap + plane))
        t[0:64, :] = mm_tn(cols[0].reshape(96, 256), put)[192:256]
        t[64:320, :] = mm_tn(cols[1].reshape(96, 256), put)
        t[320:384, :] = mm_tn(cols[2].reshape(96, 256), put)[0:64]
        every = t[...]
        moved = [every if n == 0 else pltpu.roll(every, 128 - n, 1) for n in (8 * c + a for a in range(3) for c in range(3))]
        lanes = iota((OUT1, 128), 1)
        for g in range(2):
            z = jnp.concatenate([m[OUT1 * g:OUT1 * g + 256].astype(BF) for m in moved], axis=0)
            x = mm(band1[...], z)
            row = iota((OUT1, 128), 0) + OUT1 * g
            ok = ((row >= 32) | (gy > 0)) & ((row < 288) | (gy < n_gy - 1))
            ok = ok & ((lanes > 0) | (gz > 0)) & ((lanes < 5) | (gz < n_gz - 1))
            hs[OUT1 * g:OUT1 * g + OUT1] = jnp.where(ok, jnp.maximum(x, 0.0), 0.0)

    s = sidx[...]
    s_x, s_y, s_z = s & 255, (s >> 8) & 7, s >> 11
    select_x = one_hot(rr == s_x)
    to_cy = one_hot(cc == (rr & 7) * 32 + (rr >> 3))
    acc[...] = jnp.zeros((256, 256), F32)

    def finish(z, g, x):
        at = slice(OUT2 * g, OUT2 * g + OUT2)
        made[z, at] = (x + v[z + 2, 64 + OUT2 * g:64 + OUT2 * g + OUT2, 256:512].astype(F32)).astype(BF)

    def pick(z):
        acc[...] = jnp.where(s_z == z, mm(made[z], select_x), acc[...])

    def put_out(z):
        feat[:, z] = mm(to_cy, made[z]).reshape(32, 8, 256).astype(BF)

    each_seam(-1, wait_recv)
    seams()
    each(-1, wait_recv, "row")
    for p in range(2, 6):
        widen(p)
    for q in (2, 3):
        for g in range(2):
            hide(q, g, product(band1, v, q, 0, 3, OUT1 * g))

    each(-1, wait_recv, "near", "near_corner")
    widen(1)
    widen(6)
    for q in (1, 4):
        for g in range(2):
            hide(q, g, product(band1, v, q, 0, 3, OUT1 * g))
    for i, q, lo in ((0, 0, 1), (1, 5, 0)):
        for g in range(2):
            part1[i, OUT1 * g:OUT1 * g + OUT1] = product(band1, v, q, lo, lo + 2, OUT1 * g)
    for z in (1, 2):
        for g in range(2):
            finish(z, g, product(band2, h, z, 0, 3, OUT2 * g))
    for i, z, lo in ((0, 0, 1), (1, 3, 0)):
        for g in range(2):
            part2[i, OUT2 * g:OUT2 * g + OUT2] = product(band2, h, z, lo, lo + 2, OUT2 * g)
    for z in (1, 2):
        pick(z)
        put_out(z)

    each(-1, wait_recv, "far", "far_corner")
    widen(0)
    widen(7)
    for i, q, lo in ((0, 0, 0), (1, 5, 2)):
        for g in range(2):
            hide(q, g, part1[i, OUT1 * g:OUT1 * g + OUT1] + product(band1, v, q, lo, lo + 1, OUT1 * g))
    for i, z, lo in ((0, 0, 0), (1, 3, 2)):
        for g in range(2):
            finish(z, g, part2[i, OUT2 * g:OUT2 * g + OUT2] + product(band2, h, z, lo, lo + 1, OUT2 * g))
    pick(0)
    pick(3)

    picked = jnp.where((rr >> 5) == s_y, acc[...], 0.0)
    picked = jnp.sum(picked.reshape(8, 32, 256), axis=0)
    norm = jnp.sqrt(jnp.sum(picked * picked, axis=0, keepdims=True) + 1.0)
    emb_all[0] = (picked / norm).astype(BF)

    def emb_copy(off):
        return pltpu.make_async_remote_copy(
            src_ref=emb_all.at[0], dst_ref=emb_all.at[off], send_sem=es_sem.at[off], recv_sem=er_sem.at[off],
            device_id=dev(lax.rem(gz + off, n_gz), gy, gx), device_id_type=MESH)

    for off in range(1, n_gz):
        emb_copy(off).start()
    put_out(0)
    put_out(3)

    own = emb_all[0]
    total = jnp.zeros((1, 256), F32)
    positive = jnp.zeros((1, 256), F32)
    for off in range(n_gz):
        block = lax.rem(gz + n_gz - off, n_gz)
        if off:
            emb_copy(off).wait_recv()
        e = jnp.exp(mm_tn(emb_all[off], own) * 4.0) * bm[gz, block].astype(F32)
        total = total + jnp.sum(e, axis=0, keepdims=True)
        positive = positive + jnp.sum(e * same[off], axis=0, keepdims=True)
    loss[...] = jnp.log(total) - jnp.log(positive)
    for off in range(1, n_gz):
        emb_copy(off).wait_send()
    each(1, wait_send, "near", "row", "near_corner", "far", "far_corner")
    each_seam(1, wait_send)


def shards(n_gz, n_gy, volume, first_weight, second_weight, sample_index, segments, block_match):
    vmem = pl.BlockSpec(memory_space=pltpu.VMEM)
    dma = pltpu.SemaphoreType.DMA
    features, row_loss = pl.pallas_call(
        functools.partial(kernel, n_gz, n_gy),
        out_shape=(
            jax.ShapeDtypeStruct(volume.shape, BF),
            jax.ShapeDtypeStruct((1, 256), F32),
        ),
        in_specs=[pl.BlockSpec(memory_space=pltpu.MemorySpace.HBM)] * 6,
        out_specs=(vmem, vmem),
        scratch_shapes=[
            pltpu.VMEM((4, 32, 8, 256), BF),
            pltpu.VMEM((2, 3, 3, 3, 32, 32), BF),
            pltpu.VMEM((1, 256), jnp.int32),
            pltpu.VMEM((n_gz, 1, 256), jnp.int32),
            pltpu.SMEM(block_match.shape, jnp.int32),
            pltpu.VMEM((8, 416, 768), BF),
            pltpu.VMEM((6, 384, 768), BF),
            pltpu.VMEM((OUT1, 2304), BF),
            pltpu.VMEM((OUT2, 2304), BF),
            pltpu.VMEM((2, 320, 256), F32),
            pltpu.VMEM((2, 256, 256), F32),
            pltpu.VMEM((16, 256), BF),
            pltpu.VMEM((3, 2, 3, 16, 256), BF),
            pltpu.VMEM((416, 128), F32),
            pltpu.VMEM((320, 128), F32),
            pltpu.VMEM((4, 256, 256), BF),
            pltpu.VMEM((n_gz, 256, 256), F32),
            pltpu.VMEM((n_gz, 32, 256), BF),
            pltpu.VMEM((256, 256), F32),
            dma((9,)), dma((len(HALO),)), dma((len(HALO),)), dma((len(SEAM),)), dma((len(SEAM),)), dma((n_gz,)), dma((n_gz,)),
        ],
        compiler_params=pltpu.CompilerParams(
            collective_id=0, has_side_effects=True, vmem_limit_bytes=40 << 20),
        name="voxel_contrast",
    )(
        *(pltpu.with_memory_space_constraint(a, pltpu.MemorySpace.HBM) for a in (
            volume, first_weight, second_weight, sample_index.reshape(1, 256),
            segments.reshape(segments.shape[0], 1, 256), block_match)),
    )
    return features, row_loss.reshape(1, 1, 1, 256)


def solution(mesh):
    in_specs = (
        P(None, ("group", "gz"), "gy", "gx"),
        P(),
        P(),
        P(("group", "gz"), "gy", "gx", None),
        P("group", "gy", "gx", None),
        P("group", None),
    )
    out_specs = (P(None, ("group", "gz"), "gy", "gx"), P(("group", "gz"), "gy", "gx", None))
    body = functools.partial(shards, mesh.shape["gz"], mesh.shape["gy"])
    return jax.shard_map(body, mesh=mesh, in_specs=in_specs, out_specs=out_specs, check_vma=False)
```

```python
import functools

import jax
import jax.numpy as jnp
from jax import lax
from jax.experimental import pallas as pl
from jax.experimental.pallas import tpu as pltpu
from jax.sharding import PartitionSpec as P

BF = jnp.bfloat16
F32 = jnp.float32
MESH = pl.DeviceIdType.MESH
HALO = (
    ("near", 1, 0), ("near", -1, 0), ("row", 0, 1), ("row", 0, -1),
    ("near", 1, 1), ("near", 1, -1), ("near", -1, 1), ("near", -1, -1),
    ("far", 1, 0), ("far", -1, 0),
    ("far", 1, 1), ("far", 1, -1), ("far", -1, 1), ("far", -1, -1),
)
SEAM = ((0, 1), (0, -1), (1, 0), (-1, 0), (1, 1), (1, -1), (-1, 1), (-1, -1))
NSEG = 64
PIECES1 = ((0, 64, 64), (1, 0, 0), (1, 256, 256))
PIECES2 = ((0, 0, 0), (1, 192, 192))
WIDTH, DEPTH = (256, 128), (192, 64)


def iota(shape, dim):
    return lax.broadcasted_iota(jnp.int32, shape, dim)


def mm(a, b):
    return jnp.dot(a, b, preferred_element_type=F32)


def mm_tn(a, b):
    return lax.dot_general(a, b, (((0,), (0,)), ((), ())), preferred_element_type=F32)


def mm_nt(a, b):
    return lax.dot_general(a, b, (((1,), (1,)), ((), ())), preferred_element_type=F32)


def one_hot(mask):
    return jnp.where(mask, 1.0, 0.0).astype(BF)


def kernel(n_gz, n_gy, vol_hbm, w1_hbm, w2_hbm, sidx_hbm, seg_hbm, bm_hbm, feat, loss,
           vol, wts, sidx, seg, bm, v, h, band1, band1e, band2, band2e, part1, part2, seam, cols, t, hs,
           made, same, emb_all, acc,
           in_sem, send_sem, recv_sem, ms_sem, mr_sem, ss_sem, sr_sem, es_sem, er_sem, up_sem, down_sem):
    gz, gy, gx = lax.axis_index("gz"), lax.axis_index("gy"), lax.axis_index("gx")
    other = 1 - gx

    def inside(dz, dy):
        z, y = gz + dz, gy + dy
        return (z >= 0) & (z < n_gz) & (y >= 0) & (y < n_gy)

    def dev(z, y, x):
        return {"gz": z, "gy": y, "gx": x}

    loads = [pltpu.make_async_copy(vol_hbm.at[:, z], vol.at[z], in_sem.at[z]) for z in range(4)]
    more = [
        pltpu.make_async_copy(a, b, in_sem.at[4 + i])
        for i, (a, b) in enumerate((
            (w1_hbm, wts.at[0]), (w2_hbm, wts.at[1]), (sidx_hbm, sidx), (seg_hbm, seg), (bm_hbm, bm)))
    ]
    for z in (0, 3, 1, 2):
        loads[z].start()
    for load in more:
        load.start()

    barrier = pltpu.get_barrier_semaphore()
    count = jnp.int32(1)
    pl.semaphore_signal(barrier, inc=1, device_id=dev(gz, gy, other), device_id_type=MESH)
    for dz, dy in SEAM:
        there = inside(dz, dy)
        count = count + there.astype(jnp.int32)

        @pl.when(there)
        def _():
            pl.semaphore_signal(barrier, inc=1, device_id=dev(gz + dz, gy + dy, gx), device_id_type=MESH)

    def pass_on(k):
        for sem, at, step in ((up_sem, k, 1), (down_sem, n_gz - 1 - k, -1)):
            @pl.when(gz == at)
            def _():
                if k > 0:
                    pl.semaphore_wait(sem, 1)
                if k < n_gz - 1:
                    pl.semaphore_signal(sem, inc=1, device_id=dev(gz + step, gy, gx), device_id_type=MESH)

    def rows_of(dy):
        if dy == 0:
            return slice(64, 320), slice(64, 320)
        return (slice(256, 320), slice(0, 64)) if dy == 1 else (slice(64, 128), slice(320, 384))

    def planes_of(kind, dz):
        if kind == "row":
            return slice(2, 6), slice(2, 6)
        if kind == "near":
            return (slice(5, 6), slice(1, 2)) if dz == 1 else (slice(2, 3), slice(6, 7))
        return (slice(4, 5), slice(0, 1)) if dz == 1 else (slice(3, 4), slice(7, 8))

    def halo_copy(d):
        kind, dz, dy = HALO[d]
        sr, dr = rows_of(dy)
        sp, dp = planes_of(kind, dz)
        return pltpu.make_async_remote_copy(
            src_ref=v.at[sp, sr, 256:512], dst_ref=v.at[dp, dr, 256:512], send_sem=send_sem.at[d], recv_sem=recv_sem.at[d],
            device_id=dev(gz + dz, gy + dy, gx), device_id_type=MESH)

    def mate_copy():
        return pltpu.make_async_remote_copy(
            src_ref=seam.at[0:16], dst_ref=seam.at[16:32], send_sem=ms_sem, recv_sem=mr_sem,
            device_id=dev(gz, gy, other), device_id_type=MESH)

    def seam_copy(k):
        dz, dy = SEAM[k]
        return pltpu.make_async_remote_copy(
            src_ref=seam, dst_ref=cols.at[1 - dy, 1 - dz], send_sem=ss_sem.at[k], recv_sem=sr_sem.at[k],
            device_id=dev(gz + dz, gy + dy, gx), device_id_type=MESH)

    def each(sign, act, *kinds):
        for d, (kind, dz, dy) in enumerate(HALO):
            if (kind if dy == 0 or dz == 0 else kind + "_corner") in kinds:
                @pl.when(inside(sign * dz, sign * dy))
                def _():
                    act(halo_copy(d))

    def each_seam(sign, act, first=0):
        for k, (dz, dy) in enumerate(SEAM):
            if k >= first:
                @pl.when(inside(sign * dz, sign * dy))
                def _():
                    act(seam_copy(k))

    def start(copy):
        copy.start()

    def wait_recv(copy):
        copy.wait_recv()

    def wait_send(copy):
        copy.wait_send()

    rr, cc = iota((256, 256), 0), iota((256, 256), 1)
    edge_lane = 255 * other
    side = 2 * other
    to_yc = one_hot(cc == (rr & 31) * 8 + (rr >> 5))

    def turn(z):
        loads[z].wait()
        v[z + 2, 64:320, 256:512] = mm(to_yc, vol[z].astype(F32).reshape(256, 256).astype(BF)).astype(BF)

    turn(0)
    turn(3)
    pl.semaphore_wait(barrier, count)
    pass_on(0)
    each(1, start, "near")
    turn(1)
    turn(2)
    each(1, start, "row")

    r16, l16 = iota((16, 256), 0), iota((16, 256), 1)
    lane = edge_lane + (r16 >> 2) * (1 - 2 * other)
    packed = jnp.zeros((16, 256), F32)
    for z in range(4):
        mask = (r16 < 8) & ((r16 & 3) == z) & (l16 == lane)
        packed = packed + mm_nt(one_hot(mask), v[z + 2, 64:320, 256:512])
    seam[0:16, :] = packed.astype(BF)
    mate_copy().start()
    each(1, start, "near_corner")
    pass_on(1)
    for load in more:
        load.wait()

    def build(r, band, edge):
        n_out = 6
        place = iota((32, 96), 1) - iota((32, 96), 0)
        wide = jnp.zeros((288, 96), F32)
        for b in range(3):
            wide = wide + mm(wts[r, :, b].reshape(288, 32), one_hot(place == 32 * b))
        wide = wide.astype(BF)
        tap, col = iota((96, 256 * n_out), 0), iota((96, 256 * n_out), 1)
        rows = mm(wide, one_hot(tap == (col & 255) - 32 * (col >> 8))).astype(BF)
        for y in range(n_out):
            for n in range(9):
                band[32 * y:32 * y + 32, 256 * n:256 * n + 256] = rows[32 * n:32 * n + 32, 256 * y:256 * y + 256]
                if y < 2:
                    edge[32 * y:32 * y + 32, 128 * n:128 * n + 128] = rows[32 * n:32 * n + 32, 256 * y:256 * y + 128]

    build(0, band1, band1e)
    mate_copy().wait_recv()
    each_seam(1, start)
    each(1, start, "far")
    each(1, start, "far_corner")
    for kind, dz, dy in HALO:
        @pl.when(jnp.logical_not(inside(-dz, -dy)))
        def _():
            rows, planes = rows_of(dy)[1], planes_of(kind, dz)[1]
            v[planes, rows, 256:512] = jnp.zeros((planes.stop - planes.start, rows.stop - rows.start, 256), BF)
    for dz, dy in SEAM:
        @pl.when(jnp.logical_not(inside(-dz, -dy)))
        def _():
            cols[1 - dy, 1 - dz] = jnp.zeros((32, 256), BF)
    cols[1, 1] = seam[...]
    label = iota((NSEG, 256), 0)
    own_seg = one_hot(label == seg[gz])
    for off in range(n_gz):
        block = lax.rem(gz + n_gz - off, n_gz)
        same[off] = mm_tn(one_hot(label == seg[block]), own_seg)

    def product(bands, ref, p, lo, hi, piece):
        edge, first, _ = piece
        n = WIDTH[edge]
        rhs = [ref[p + i, first:first + n, 256 * c:256 * c + 256] for i in range(lo, hi) for c in range(3)]
        return mm(bands[edge][:, 3 * n * lo:3 * n * hi], jnp.concatenate(rhs, axis=0))

    def rows_out(piece):
        return slice(piece[2], piece[2] + DEPTH[piece[0]])

    def widened(x, col):
        lanes = iota(x.shape, 1)
        left = jnp.where(lanes == 0, jnp.where(gx == 1, col, 0.0), pltpu.roll(x, 1, 1))
        right = jnp.where(lanes == 255, jnp.where(gx == 0, col, 0.0), pltpu.roll(x, 255, 1))
        return left.astype(BF), right.astype(BF)

    def widen(p, first, last):
        at = slice(first, last)
        x = v[p, at, 256:512].astype(F32)
        v[p, at, 0:256], v[p, at, 512:768] = widened(x, t[at, 8 + p:9 + p])

    def valid(shape, q, first):
        row = iota(shape, 0) + first
        ok = ((row >= 32) | (gy > 0)) & ((row < 288) | (gy < n_gy - 1))
        return ok & ((q > 0) | (gz > 0)) & ((q < 5) | (gz < n_gz - 1))

    def hide(q, piece, x, seamed):
        at = rows_out(piece)
        x = jnp.where(valid(x.shape, q, at.start), jnp.maximum(x, 0.0), 0.0)
        h[q, at, 256:512] = x.astype(BF)
        h[q, at, 0:256], h[q, at, 512:768] = widened(x, hs[at, q:q + 1] if seamed else 0.0)

    def insert_seam(q):
        lanes = iota((320, 128), 1)
        for x, lane, at in ((0, 127, slice(640, 768)), (1, 0, slice(0, 128))):
            @pl.when(gx == x)
            def _():
                old = h[q, 0:320, at].astype(F32)
                h[q, 0:320, at] = jnp.where(lanes == lane, hs[:, q:q + 1], old).astype(BF)

    row, col = iota((96, 128), 0), iota((96, 128), 1)
    core = (row >> 4) & 1
    j = (row & 15) >> 2
    plane = (row & 3) + 4 * (row >> 5) - 2
    tap = jnp.where(core == 0, 2 - side, jnp.where(j == 0, 1, side))
    put = one_hot((j + (1 - core) < 2) & (plane >= 0) & (plane < 8) & (col == 8 * tap + plane))

    def unpack(dy, picked, n):
        to, rows = ((slice(0, 64), slice(192, 256)), (slice(64, 320), slice(0, 256)), (slice(320, 384), slice(0, 64)))[dy]
        placed = mm_tn(cols[dy, picked].reshape(32 * n, 256), put[32 * picked.start:32 * picked.stop])
        t[to, :] = placed[rows]

    def seams():
        every = t[...]
        moved = [every if n == 0 else pltpu.roll(every, 128 - n, 1) for n in (8 * c + a for a in range(3) for c in range(3))]
        for piece in PIECES1:
            edge, first, out = piece
            n = DEPTH[edge]
            z = jnp.concatenate([m[first:first + WIDTH[edge]].astype(BF) for m in moved], axis=0)
            x = mm(bands1[edge][...], z)
            row, lanes = iota((n, 128), 0) + out, iota((n, 128), 1)
            ok = ((row >= 32) | (gy > 0)) & ((row < 288) | (gy < n_gy - 1))
            ok = ok & ((lanes > 0) | (gz > 0)) & ((lanes < 5) | (gz < n_gz - 1))
            hs[out:out + n] = jnp.where(ok, jnp.maximum(x, 0.0), 0.0)

    s = sidx[...]
    s_x, s_y, s_z = s & 255, (s >> 8) & 7, s >> 11
    select_x = one_hot(rr == s_x)
    to_cy = one_hot(cc == (rr & 7) * 32 + (rr >> 3))
    acc[...] = jnp.zeros((256, 256), F32)

    def finish(z, piece, x):
        at = rows_out(piece)
        made[z, at] = (x + v[z + 2, 64 + at.start:64 + at.stop, 256:512].astype(F32)).astype(BF)

    def pick(z):
        acc[...] = jnp.where(s_z == z, mm(made[z], select_x), acc[...])

    def put_out(z):
        feat[:, z] = mm(to_cy, made[z]).reshape(32, 8, 256).astype(BF)

    bands1, bands2 = (band1, band1e), (band2, band2e)
    middle, edges = PIECES1[0], PIECES1[1:]

    unpack(1, slice(1, 2), 1)
    for p in range(2, 6):
        widen(p, 64, 320)
    for q in (2, 3):
        hide(q, middle, product(bands1, v, q, 0, 3, middle), False)
    for q, lo, hi in ((1, 1, 3), (4, 0, 2), (0, 2, 3), (5, 0, 1)):
        part1[q, rows_out(middle)] = product(bands1, v, q, lo, hi, middle)
    for k in range(2, min(3, n_gz)):
        pass_on(k)
    build(1, band2, band2e)
    for k in range(3, n_gz):
        pass_on(k)

    each(-1, wait_recv, "row")
    for k in (0, 1):
        @pl.when(inside(*(-d for d in SEAM[k])))
        def _():
            seam_copy(k).wait_recv()
    for dy in (0, 2):
        unpack(dy, slice(1, 2), 1)
    for p in range(2, 6):
        widen(p, 0, 64)
        widen(p, 320, 384)
    for q in (2, 3):
        for piece in edges:
            hide(q, piece, product(bands1, v, q, 0, 3, piece), False)

    each(-1, wait_recv, "near", "near_corner")
    each_seam(-1, wait_recv, 2)
    for dy in range(3):
        unpack(dy, slice(0, 3), 3)
    seams()
    insert_seam(2)
    insert_seam(3)
    for p in (1, 6):
        widen(p, 0, 384)
    for q, lo in ((1, 0), (4, 2)):
        hide(q, middle, part1[q, rows_out(middle)] + product(bands1, v, q, lo, lo + 1, middle), True)
        for piece in edges:
            hide(q, piece, product(bands1, v, q, 0, 3, piece), True)
    for q, lo in ((0, 1), (5, 0)):
        at = rows_out(middle)
        part1[q, at] = part1[q, at] + product(bands1, v, q, 1, 2, middle)
        for piece in edges:
            part1[q, rows_out(piece)] = product(bands1, v, q, lo, lo + 2, piece)
    for z in (1, 2):
        for piece in PIECES2:
            finish(z, piece, product(bands2, h, z, 0, 3, piece))
    for i, z, lo in ((0, 0, 1), (1, 3, 0)):
        for piece in PIECES2:
            part2[i, rows_out(piece)] = product(bands2, h, z, lo, lo + 2, piece)
    for z in (1, 2):
        pick(z)
        put_out(z)

    each(-1, wait_recv, "far", "far_corner")
    for p in (0, 7):
        widen(p, 0, 384)
    for q, lo in ((0, 0), (5, 2)):
        for piece in PIECES1:
            hide(q, piece, part1[q, rows_out(piece)] + product(bands1, v, q, lo, lo + 1, piece), True)
    for i, z, lo in ((0, 0, 0), (1, 3, 2)):
        for piece in PIECES2:
            finish(z, piece, part2[i, rows_out(piece)] + product(bands2, h, z, lo, lo + 1, piece))
    pick(0)
    pick(3)

    picked = jnp.where((rr >> 5) == s_y, acc[...], 0.0)
    picked = jnp.sum(picked.reshape(8, 32, 256), axis=0)
    norm = jnp.sqrt(jnp.sum(picked * picked, axis=0, keepdims=True) + 1.0)
    emb_all[0] = (picked / norm).astype(BF)

    def emb_copy(off):
        return pltpu.make_async_remote_copy(
            src_ref=emb_all.at[0], dst_ref=emb_all.at[off], send_sem=es_sem.at[off], recv_sem=er_sem.at[off],
            device_id=dev(lax.rem(gz + off, n_gz), gy, gx), device_id_type=MESH)

    for off in range(1, n_gz):
        emb_copy(off).start()
    put_out(0)
    put_out(3)

    own = emb_all[0]
    total = jnp.zeros((1, 256), F32)
    positive = jnp.zeros((1, 256), F32)
    for off in range(n_gz):
        block = lax.rem(gz + n_gz - off, n_gz)
        if off:
            emb_copy(off).wait_recv()
        e = jnp.exp(mm_tn(emb_all[off], own) * 4.0) * bm[gz, block].astype(F32)
        total = total + jnp.sum(e, axis=0, keepdims=True)
        positive = positive + jnp.sum(e * same[off], axis=0, keepdims=True)
    loss[...] = jnp.log(total) - jnp.log(positive)
    for off in range(1, n_gz):
        emb_copy(off).wait_send()
    each(1, wait_send, "near", "row", "near_corner", "far", "far_corner")
    each_seam(1, wait_send)
    mate_copy().wait_send()


def write_out(feat, loss, feat_hbm, loss_hbm, sem):
    copies = [pltpu.make_async_copy(feat, feat_hbm, sem.at[0]), pltpu.make_async_copy(loss, loss_hbm, sem.at[1])]
    for copy in copies:
        copy.start()
    for copy in copies:
        copy.wait()


def shards(n_gz, n_gy, volume, first_weight, second_weight, sample_index, segments, block_match):
    vmem = pl.BlockSpec(memory_space=pltpu.VMEM)
    dma = pltpu.SemaphoreType.DMA
    features, row_loss = pl.pallas_call(
        functools.partial(kernel, n_gz, n_gy),
        out_shape=(
            jax.ShapeDtypeStruct(volume.shape, BF),
            jax.ShapeDtypeStruct((1, 256), F32),
        ),
        in_specs=[pl.BlockSpec(memory_space=pltpu.MemorySpace.HBM)] * 6,
        out_specs=(vmem, vmem),
        scratch_shapes=[
            pltpu.VMEM((4, 32, 8, 256), BF),
            pltpu.VMEM((2, 3, 3, 3, 32, 32), BF),
            pltpu.VMEM((1, 256), jnp.int32),
            pltpu.VMEM((n_gz, 1, 256), jnp.int32),
            pltpu.SMEM(block_match.shape, jnp.int32),
            pltpu.VMEM((8, 384, 768), BF),
            pltpu.VMEM((6, 320, 768), BF),
            pltpu.VMEM((192, 2304), BF),
            pltpu.VMEM((64, 1152), BF),
            pltpu.VMEM((192, 2304), BF),
            pltpu.VMEM((64, 1152), BF),
            pltpu.VMEM((6, 320, 256), F32),
            pltpu.VMEM((2, 256, 256), F32),
            pltpu.VMEM((32, 256), BF),
            pltpu.VMEM((3, 3, 32, 256), BF),
            pltpu.VMEM((384, 128), F32),
            pltpu.VMEM((320, 128), F32),
            pltpu.VMEM((4, 256, 256), BF),
            pltpu.VMEM((n_gz, 256, 256), F32),
            pltpu.VMEM((n_gz, 32, 256), BF),
            pltpu.VMEM((256, 256), F32),
            dma((9,)), dma((len(HALO),)), dma((len(HALO),)), dma, dma, dma((len(SEAM),)), dma((len(SEAM),)), dma((n_gz,)), dma((n_gz,)),
            pltpu.SemaphoreType.REGULAR, pltpu.SemaphoreType.REGULAR,
        ],
        compiler_params=pltpu.CompilerParams(
            collective_id=0, has_side_effects=True, vmem_limit_bytes=40 << 20),
        name="voxel_contrast",
    )(
        *(pltpu.with_memory_space_constraint(a, pltpu.MemorySpace.HBM) for a in (
            volume, first_weight, second_weight, sample_index.reshape(1, 256),
            segments.reshape(segments.shape[0], 1, 256), block_match)),
    )
    hbm = pl.BlockSpec(memory_space=pltpu.MemorySpace.HBM)
    features, row_loss = pl.pallas_call(
        write_out,
        out_shape=(jax.ShapeDtypeStruct(volume.shape, BF), jax.ShapeDtypeStruct((1, 256), F32)),
        in_specs=[vmem, vmem],
        out_specs=(hbm, hbm),
        scratch_shapes=[dma((2,))],
        name="write_out",
    )(*(pltpu.with_memory_space_constraint(a, pltpu.MemorySpace.VMEM) for a in (features, row_loss)))
    return features, row_loss.reshape(1, 1, 1, 256)


def solution(mesh):
    in_specs = (
        P(None, ("group", "gz"), "gy", "gx"),
        P(),
        P(),
        P(("group", "gz"), "gy", "gx", None),
        P("group", "gy", "gx", None),
        P("group", None),
    )
    out_specs = (P(None, ("group", "gz"), "gy", "gx"), P(("group", "gz"), "gy", "gx", None))
    body = functools.partial(shards, mesh.shape["gz"], mesh.shape["gy"])
    return jax.shard_map(body, mesh=mesh, in_specs=in_specs, out_specs=out_specs, check_vma=False)
```

```python
import functools

import jax
import jax.numpy as jnp
from jax import lax
from jax.experimental import pallas as pl
from jax.experimental.pallas import tpu as pltpu
from jax.sharding import PartitionSpec as P

BF = jnp.bfloat16
F32 = jnp.float32
MESH = pl.DeviceIdType.MESH
HALO = (
    ("near", 1, 0), ("near", -1, 0), ("row", 0, 1), ("row", 0, -1),
    ("near", 1, 1), ("near", 1, -1), ("near", -1, 1), ("near", -1, -1),
    ("far", 1, 0), ("far", -1, 0),
    ("far", 1, 1), ("far", 1, -1), ("far", -1, 1), ("far", -1, -1),
)
SEAM = ((0, 1), (0, -1), (1, 0), (-1, 0), (1, 1), (1, -1), (-1, 1), (-1, -1))
NSEG = 64
PIECES1 = ((0, 64, 64), (1, 0, 0), (1, 256, 256))
PIECES2 = ((0, 0, 0), (1, 192, 192))
WIDTH, DEPTH = (256, 128), (192, 64)


def iota(shape, dim):
    return lax.broadcasted_iota(jnp.int32, shape, dim)


def mm(a, b):
    return jnp.dot(a, b, preferred_element_type=F32)


def mm_tn(a, b):
    return lax.dot_general(a, b, (((0,), (0,)), ((), ())), preferred_element_type=F32)


def mm_nt(a, b):
    return lax.dot_general(a, b, (((1,), (1,)), ((), ())), preferred_element_type=F32)


def one_hot(mask):
    return jnp.where(mask, 1.0, 0.0).astype(BF)


def kernel(n_gz, n_gy, vol_hbm, w1_hbm, w2_hbm, sidx_hbm, seg_hbm, bm_hbm, feat, loss,
           vol, wts, sidx, seg, bm, v, h, band1, band1e, band2, band2e, part1, part2, own_cols, mate_cols, seam, cols, t, hs,
           made, same, emb_all, acc,
           in_sem, send_sem, recv_sem, ms_sem, mr_sem, ss_sem, sr_sem, es_sem, er_sem, up_sem, down_sem):
    gz, gy, gx = lax.axis_index("gz"), lax.axis_index("gy"), lax.axis_index("gx")
    other = 1 - gx

    def inside(dz, dy):
        z, y = gz + dz, gy + dy
        return (z >= 0) & (z < n_gz) & (y >= 0) & (y < n_gy)

    def dev(z, y, x):
        return {"gz": z, "gy": y, "gx": x}

    loads = [pltpu.make_async_copy(vol_hbm.at[:, z], vol.at[z], in_sem.at[z]) for z in range(4)]
    more = [
        pltpu.make_async_copy(a, b, in_sem.at[4 + i])
        for i, (a, b) in enumerate((
            (w1_hbm, wts.at[0]), (w2_hbm, wts.at[1]), (sidx_hbm, sidx), (seg_hbm, seg), (bm_hbm, bm)))
    ]
    for z in (0, 3, 1, 2):
        loads[z].start()
    for load in more:
        load.start()

    barrier = pltpu.get_barrier_semaphore()
    count = jnp.int32(1)
    pl.semaphore_signal(barrier, inc=1, device_id=dev(gz, gy, other), device_id_type=MESH)
    for dz, dy in SEAM:
        there = inside(dz, dy)
        count = count + there.astype(jnp.int32)

        @pl.when(there)
        def _():
            pl.semaphore_signal(barrier, inc=1, device_id=dev(gz + dz, gy + dy, gx), device_id_type=MESH)

    def pass_on(k):
        for sem, at, step in ((up_sem, k, 1), (down_sem, n_gz - 1 - k, -1)):
            @pl.when(gz == at)
            def _():
                if k > 0:
                    pl.semaphore_wait(sem, 1)
                if k < n_gz - 1:
                    pl.semaphore_signal(sem, inc=1, device_id=dev(gz + step, gy, gx), device_id_type=MESH)

    def rows_of(dy):
        if dy == 0:
            return slice(64, 320), slice(64, 320)
        return (slice(256, 320), slice(0, 64)) if dy == 1 else (slice(64, 128), slice(320, 384))

    def planes_of(kind, dz):
        if kind == "row":
            return slice(2, 6), slice(2, 6)
        if kind == "near":
            return (slice(5, 6), slice(1, 2)) if dz == 1 else (slice(2, 3), slice(6, 7))
        return (slice(4, 5), slice(0, 1)) if dz == 1 else (slice(3, 4), slice(7, 8))

    def halo_copy(d):
        kind, dz, dy = HALO[d]
        sr, dr = rows_of(dy)
        sp, dp = planes_of(kind, dz)
        return pltpu.make_async_remote_copy(
            src_ref=v.at[sp, sr, 256:512], dst_ref=v.at[dp, dr, 256:512], send_sem=send_sem.at[d], recv_sem=recv_sem.at[d],
            device_id=dev(gz + dz, gy + dy, gx), device_id_type=MESH)

    def mate_copy():
        return pltpu.make_async_remote_copy(
            src_ref=own_cols, dst_ref=mate_cols, send_sem=ms_sem, recv_sem=mr_sem,
            device_id=dev(gz, gy, other), device_id_type=MESH)

    def seam_copy(k):
        dz, dy = SEAM[k]
        part = (slice(0, 256), slice(128, 256), slice(0, 128))[dy]
        return pltpu.make_async_remote_copy(
            src_ref=seam.at[:, part], dst_ref=cols.at[1 - dy, 1 - dz, :, part], send_sem=ss_sem.at[k], recv_sem=sr_sem.at[k],
            device_id=dev(gz + dz, gy + dy, gx), device_id_type=MESH)

    def each(sign, act, *kinds):
        for d, (kind, dz, dy) in enumerate(HALO):
            if (kind if dy == 0 or dz == 0 else kind + "_corner") in kinds:
                @pl.when(inside(sign * dz, sign * dy))
                def _():
                    act(halo_copy(d))

    def each_seam(sign, act, first=0):
        for k, (dz, dy) in enumerate(SEAM):
            if k >= first:
                @pl.when(inside(sign * dz, sign * dy))
                def _():
                    act(seam_copy(k))

    def start(copy):
        copy.start()

    def wait_recv(copy):
        copy.wait_recv()

    def wait_send(copy):
        copy.wait_send()

    rr, cc = iota((256, 256), 0), iota((256, 256), 1)
    edge_lane = 255 * other
    side = 2 * other
    to_yc = one_hot(cc == (rr & 31) * 8 + (rr >> 5))

    def turn(z):
        loads[z].wait()
        v[z + 2, 64:320, 256:512] = mm(to_yc, vol[z].astype(F32).reshape(256, 256).astype(BF)).astype(BF)

    turn(0)
    turn(3)
    pl.semaphore_wait(barrier, count)
    pass_on(0)
    each(1, start, "near")
    turn(1)
    turn(2)
    each(1, start, "row")

    r16, l16 = iota((16, 256), 0), iota((16, 256), 1)
    lane = edge_lane + ((r16 >> 2) & 1) * (1 - 2 * other)
    packed = jnp.zeros((16, 256), F32)
    for z in range(4):
        mask = ((r16 & 3) == z) & (l16 == lane)
        packed = packed + mm_nt(one_hot(mask), v[z + 2, 64:320, 256:512])
    own_cols[...] = packed.astype(BF)
    mate_copy().start()
    each(1, start, "near_corner")
    pass_on(1)
    for load in more:
        load.wait()

    def build(r, band, edge):
        n_out = 6
        place = iota((32, 96), 1) - iota((32, 96), 0)
        wide = jnp.zeros((288, 96), F32)
        for b in range(3):
            wide = wide + mm(wts[r, :, b].reshape(288, 32), one_hot(place == 32 * b))
        wide = wide.astype(BF)
        tap, col = iota((96, 256 * n_out), 0), iota((96, 256 * n_out), 1)
        rows = mm(wide, one_hot(tap == (col & 255) - 32 * (col >> 8))).astype(BF)
        for y in range(n_out):
            for n in range(9):
                band[32 * y:32 * y + 32, 256 * n:256 * n + 256] = rows[32 * n:32 * n + 32, 256 * y:256 * y + 256]
                if y < 2:
                    edge[32 * y:32 * y + 32, 128 * n:128 * n + 128] = rows[32 * n:32 * n + 32, 256 * y:256 * y + 128]

    build(0, band1, band1e)
    mate_copy().wait_recv()
    both = jnp.where(r16 < 8, own_cols[...].astype(F32), mate_cols[...].astype(F32)).astype(BF)
    seam[...] = both
    each_seam(1, start)
    each(1, start, "far")
    each(1, start, "far_corner")
    for kind, dz, dy in HALO:
        @pl.when(jnp.logical_not(inside(-dz, -dy)))
        def _():
            rows, planes = rows_of(dy)[1], planes_of(kind, dz)[1]
            v[planes, rows, 256:512] = jnp.zeros((planes.stop - planes.start, rows.stop - rows.start, 256), BF)
    for dz, dy in SEAM:
        @pl.when(jnp.logical_not(inside(-dz, -dy)))
        def _():
            cols[1 - dy, 1 - dz] = jnp.zeros((16, 256), BF)
    cols[1, 1] = both
    label = iota((NSEG, 256), 0)
    own_seg = one_hot(label == seg[gz])
    for off in range(n_gz):
        block = lax.rem(gz + n_gz - off, n_gz)
        same[off] = mm_tn(one_hot(label == seg[block]), own_seg)

    def product(bands, ref, p, lo, hi, piece):
        edge, first, _ = piece
        n = WIDTH[edge]
        rhs = [ref[p + i, first:first + n, 256 * c:256 * c + 256] for i in range(lo, hi) for c in range(3)]
        return mm(bands[edge][:, 3 * n * lo:3 * n * hi], jnp.concatenate(rhs, axis=0))

    def rows_out(piece):
        return slice(piece[2], piece[2] + DEPTH[piece[0]])

    def widened(x, col):
        lanes = iota(x.shape, 1)
        left = jnp.where(lanes == 0, jnp.where(gx == 1, col, 0.0), pltpu.roll(x, 1, 1))
        right = jnp.where(lanes == 255, jnp.where(gx == 0, col, 0.0), pltpu.roll(x, 255, 1))
        return left.astype(BF), right.astype(BF)

    def widen(p, first, last):
        at = slice(first, last)
        x = v[p, at, 256:512].astype(F32)
        v[p, at, 0:256], v[p, at, 512:768] = widened(x, t[at, 8 + p:9 + p])

    def valid(shape, q, first):
        row = iota(shape, 0) + first
        ok = ((row >= 32) | (gy > 0)) & ((row < 288) | (gy < n_gy - 1))
        return ok & ((q > 0) | (gz > 0)) & ((q < 5) | (gz < n_gz - 1))

    def hide(q, piece, x, seamed):
        at = rows_out(piece)
        x = jnp.where(valid(x.shape, q, at.start), jnp.maximum(x, 0.0), 0.0)
        h[q, at, 256:512] = x.astype(BF)
        h[q, at, 0:256], h[q, at, 512:768] = widened(x, hs[at, q:q + 1] if seamed else 0.0)

    def insert_seam(q):
        lanes = iota((320, 128), 1)
        for x, lane, at in ((0, 127, slice(640, 768)), (1, 0, slice(0, 128))):
            old = h[q, 0:320, at].astype(F32)
            h[q, 0:320, at] = jnp.where((lanes == lane) & (gx == x), hs[:, q:q + 1], old).astype(BF)

    row, col = iota((48, 128), 0), iota((48, 128), 1)
    core = (row >> 3) & 1
    j = (row >> 2) & 1
    plane = (row & 3) + 4 * (row >> 4) - 2
    tap = jnp.where(core == 0, 2 - side, jnp.where(j == 0, 1, side))
    put = one_hot((j + (1 - core) < 2) & (plane >= 0) & (plane < 8) & (col == 8 * tap + plane))

    def unpack(dy, picked, n):
        to, part, rows = (
            (slice(0, 64), slice(128, 256), slice(64, 128)),
            (slice(64, 320), slice(0, 256), slice(0, 256)),
            (slice(320, 384), slice(0, 128), slice(0, 64)))[dy]
        packed = cols[dy, picked, :, part]
        placed = mm_tn(packed.reshape(16 * n, part.stop - part.start), put[16 * picked.start:16 * picked.stop])
        t[to, :] = placed[rows]

    def seams():
        every = t[...]
        moved = [every if n == 0 else pltpu.roll(every, 128 - n, 1) for n in (8 * c + a for a in range(3) for c in range(3))]
        for piece in PIECES1:
            edge, first, out = piece
            n = DEPTH[edge]
            z = jnp.concatenate([m[first:first + WIDTH[edge]].astype(BF) for m in moved], axis=0)
            x = mm(bands1[edge][...], z)
            row, lanes = iota((n, 128), 0) + out, iota((n, 128), 1)
            ok = ((row >= 32) | (gy > 0)) & ((row < 288) | (gy < n_gy - 1))
            ok = ok & ((lanes > 0) | (gz > 0)) & ((lanes < 5) | (gz < n_gz - 1))
            hs[out:out + n] = jnp.where(ok, jnp.maximum(x, 0.0), 0.0)

    s = sidx[...]
    s_x, s_y, s_z = s & 255, (s >> 8) & 7, s >> 11
    select_x = one_hot(rr == s_x)
    to_cy = one_hot(cc == (rr & 7) * 32 + (rr >> 3))
    acc[...] = jnp.zeros((256, 256), F32)

    def finish(z, piece, x):
        at = rows_out(piece)
        made[z, at] = (x + v[z + 2, 64 + at.start:64 + at.stop, 256:512].astype(F32)).astype(BF)

    def pick(z):
        acc[...] = jnp.where(s_z == z, mm(made[z], select_x), acc[...])

    def put_out(z):
        feat[:, z] = mm(to_cy, made[z]).reshape(32, 8, 256).astype(BF)

    bands1, bands2 = (band1, band1e), (band2, band2e)
    middle, edges = PIECES1[0], PIECES1[1:]

    unpack(1, slice(1, 2), 1)
    for p in range(2, 6):
        widen(p, 64, 320)
    for q in (2, 3):
        hide(q, middle, product(bands1, v, q, 0, 3, middle), False)
    for q, lo, hi in ((1, 1, 3), (4, 0, 2), (0, 2, 3), (5, 0, 1)):
        part1[q, rows_out(middle)] = product(bands1, v, q, lo, hi, middle)
    for k in range(2, min(3, n_gz)):
        pass_on(k)
    build(1, band2, band2e)
    for k in range(3, n_gz):
        pass_on(k)

    each(-1, wait_recv, "row")
    for k in (0, 1):
        @pl.when(inside(*(-d for d in SEAM[k])))
        def _():
            seam_copy(k).wait_recv()
    for dy in (0, 2):
        unpack(dy, slice(1, 2), 1)
    for p in range(2, 6):
        widen(p, 0, 64)
        widen(p, 320, 384)
    for q in (2, 3):
        for piece in edges:
            hide(q, piece, product(bands1, v, q, 0, 3, piece), False)
    for q, lo, hi in ((1, 1, 3), (4, 0, 2), (0, 2, 3), (5, 0, 1)):
        for piece in edges:
            part1[q, rows_out(piece)] = product(bands1, v, q, lo, hi, piece)

    each(-1, wait_recv, "near", "near_corner")
    each_seam(-1, wait_recv, 2)
    for dy in range(3):
        unpack(dy, slice(0, 3), 3)
    for p in (1, 6):
        widen(p, 0, 384)
    for q, lo in ((1, 0), (4, 2)):
        for piece in PIECES1:
            hide(q, piece, part1[q, rows_out(piece)] + product(bands1, v, q, lo, lo + 1, piece), False)
    seams()
    for q in range(1, 5):
        insert_seam(q)
    for q in (0, 5):
        for piece in PIECES1:
            at = rows_out(piece)
            part1[q, at] = part1[q, at] + product(bands1, v, q, 1, 2, piece)
    for z in (1, 2):
        for piece in PIECES2:
            finish(z, piece, product(bands2, h, z, 0, 3, piece))
    for i, z, lo in ((0, 0, 1), (1, 3, 0)):
        for piece in PIECES2:
            part2[i, rows_out(piece)] = product(bands2, h, z, lo, lo + 2, piece)
    for z in (1, 2):
        pick(z)
        put_out(z)

    each(-1, wait_recv, "far", "far_corner")
    for p in (0, 7):
        widen(p, 0, 384)
    for q, lo in ((0, 0), (5, 2)):
        for piece in PIECES1:
            hide(q, piece, part1[q, rows_out(piece)] + product(bands1, v, q, lo, lo + 1, piece), True)
    for i, z, lo in ((0, 0, 0), (1, 3, 2)):
        for piece in PIECES2:
            finish(z, piece, part2[i, rows_out(piece)] + product(bands2, h, z, lo, lo + 1, piece))
    pick(0)
    pick(3)

    picked = jnp.where((rr >> 5) == s_y, acc[...], 0.0)
    picked = jnp.sum(picked.reshape(8, 32, 256), axis=0)
    norm = jnp.sqrt(jnp.sum(picked * picked, axis=0, keepdims=True) + 1.0)
    emb_all[0] = (picked / norm).astype(BF)

    def emb_copy(off):
        return pltpu.make_async_remote_copy(
            src_ref=emb_all.at[0], dst_ref=emb_all.at[off], send_sem=es_sem.at[off], recv_sem=er_sem.at[off],
            device_id=dev(lax.rem(gz + off, n_gz), gy, gx), device_id_type=MESH)

    for k in range(1, n_gz):
        emb_copy(jnp.where(2 * gz < n_gz, n_gz - k, k)).start()
    put_out(0)
    put_out(3)

    own = emb_all[0]
    total = jnp.zeros((1, 256), F32)
    positive = jnp.zeros((1, 256), F32)
    for off in range(n_gz):
        block = lax.rem(gz + n_gz - off, n_gz)
        if off:
            emb_copy(off).wait_recv()
        e = jnp.exp(mm_tn(emb_all[off], own) * 4.0) * bm[gz, block].astype(F32)
        total = total + jnp.sum(e, axis=0, keepdims=True)
        positive = positive + jnp.sum(e * same[off], axis=0, keepdims=True)
    loss[...] = jnp.log(total) - jnp.log(positive)
    for off in range(1, n_gz):
        emb_copy(off).wait_send()
    each(1, wait_send, "near", "row", "near_corner", "far", "far_corner")
    each_seam(1, wait_send)
    mate_copy().wait_send()


def write_out(feat, loss, feat_hbm, loss_hbm, sem):
    copies = [pltpu.make_async_copy(feat, feat_hbm, sem.at[0]), pltpu.make_async_copy(loss, loss_hbm, sem.at[1])]
    for copy in copies:
        copy.start()
    for copy in copies:
        copy.wait()


def shards(n_gz, n_gy, volume, first_weight, second_weight, sample_index, segments, block_match):
    vmem = pl.BlockSpec(memory_space=pltpu.VMEM)
    dma = pltpu.SemaphoreType.DMA
    features, row_loss = pl.pallas_call(
        functools.partial(kernel, n_gz, n_gy),
        out_shape=(
            jax.ShapeDtypeStruct(volume.shape, BF),
            jax.ShapeDtypeStruct((1, 256), F32),
        ),
        in_specs=[pl.BlockSpec(memory_space=pltpu.MemorySpace.HBM)] * 6,
        out_specs=(vmem, vmem),
        scratch_shapes=[
            pltpu.VMEM((4, 32, 8, 256), BF),
            pltpu.VMEM((2, 3, 3, 3, 32, 32), BF),
            pltpu.VMEM((1, 256), jnp.int32),
            pltpu.VMEM((n_gz, 1, 256), jnp.int32),
            pltpu.SMEM(block_match.shape, jnp.int32),
            pltpu.VMEM((8, 384, 768), BF),
            pltpu.VMEM((6, 320, 768), BF),
            pltpu.VMEM((192, 2304), BF),
            pltpu.VMEM((64, 1152), BF),
            pltpu.VMEM((192, 2304), BF),
            pltpu.VMEM((64, 1152), BF),
            pltpu.VMEM((6, 320, 256), F32),
            pltpu.VMEM((2, 256, 256), F32),
            pltpu.VMEM((16, 256), BF),
            pltpu.VMEM((16, 256), BF),
            pltpu.VMEM((16, 256), BF),
            pltpu.VMEM((3, 3, 16, 256), BF),
            pltpu.VMEM((384, 128), F32),
            pltpu.VMEM((320, 128), F32),
            pltpu.VMEM((4, 256, 256), BF),
            pltpu.VMEM((n_gz, 256, 256), F32),
            pltpu.VMEM((n_gz, 32, 256), BF),
            pltpu.VMEM((256, 256), F32),
            dma((9,)), dma((len(HALO),)), dma((len(HALO),)), dma, dma, dma((len(SEAM),)), dma((len(SEAM),)), dma((n_gz,)), dma((n_gz,)),
            pltpu.SemaphoreType.REGULAR, pltpu.SemaphoreType.REGULAR,
        ],
        compiler_params=pltpu.CompilerParams(
            collective_id=0, has_side_effects=True, vmem_limit_bytes=40 << 20),
        name="voxel_contrast",
    )(
        *(pltpu.with_memory_space_constraint(a, pltpu.MemorySpace.HBM) for a in (
            volume, first_weight, second_weight, sample_index.reshape(1, 256),
            segments.reshape(segments.shape[0], 1, 256), block_match)),
    )
    hbm = pl.BlockSpec(memory_space=pltpu.MemorySpace.HBM)
    features, row_loss = pl.pallas_call(
        write_out,
        out_shape=(jax.ShapeDtypeStruct(volume.shape, BF), jax.ShapeDtypeStruct((1, 256), F32)),
        in_specs=[vmem, vmem],
        out_specs=(hbm, hbm),
        scratch_shapes=[dma((2,))],
        name="write_out",
    )(*(pltpu.with_memory_space_constraint(a, pltpu.MemorySpace.VMEM) for a in (features, row_loss)))
    return features, row_loss.reshape(1, 1, 1, 256)


def solution(mesh):
    in_specs = (
        P(None, ("group", "gz"), "gy", "gx"),
        P(),
        P(),
        P(("group", "gz"), "gy", "gx", None),
        P("group", "gy", "gx", None),
        P("group", None),
    )
    out_specs = (P(None, ("group", "gz"), "gy", "gx"), P(("group", "gz"), "gy", "gx", None))
    body = functools.partial(shards, mesh.shape["gz"], mesh.shape["gy"])
    return jax.shard_map(body, mesh=mesh, in_specs=in_specs, out_specs=out_specs, check_vma=False)
```

```python
import functools

import jax
import jax.numpy as jnp
from jax import lax
from jax.experimental import pallas as pl
from jax.experimental.pallas import tpu as pltpu
from jax.sharding import PartitionSpec as P

BF = jnp.bfloat16
F32 = jnp.float32
MESH = pl.DeviceIdType.MESH
HALO = (
    ("near", 1, 0), ("near", -1, 0), ("row", 0, 1), ("row", 0, -1),
    ("near", 1, 1), ("near", 1, -1), ("near", -1, 1), ("near", -1, -1),
    ("far", 1, 0), ("far", -1, 0),
    ("far", 1, 1), ("far", 1, -1), ("far", -1, 1), ("far", -1, -1),
)
SEAM = ((0, 1), (0, -1), (1, 0), (-1, 0), (1, 1), (1, -1), (-1, 1), (-1, -1))
NSEG = 64
PIECES1 = ((0, 64, 64), (1, 0, 0), (1, 256, 256))
PIECES2 = ((0, 0, 0), (1, 192, 192))
WIDTH, DEPTH = (256, 128), (192, 64)


def iota(shape, dim):
    return lax.broadcasted_iota(jnp.int32, shape, dim)


def mm(a, b):
    return jnp.dot(a, b, preferred_element_type=F32)


def mm_tn(a, b):
    return lax.dot_general(a, b, (((0,), (0,)), ((), ())), preferred_element_type=F32)


def mm_nt(a, b):
    return lax.dot_general(a, b, (((1,), (1,)), ((), ())), preferred_element_type=F32)


def one_hot(mask):
    return jnp.where(mask, 1.0, 0.0).astype(BF)


def kernel(n_gz, n_gy, vol_hbm, w1_hbm, w2_hbm, sidx_hbm, seg_hbm, bm_hbm, feat, loss,
           vol, wts, sidx, seg, bm, v, h, band1, band1e, band2, band2e, part1, part2, own_cols, mate_cols, seam, cols, t, hs,
           made, same, emb_all, acc,
           in_sem, send_sem, recv_sem, ms_sem, mr_sem, ss_sem, sr_sem, es_sem, er_sem, up_sem, down_sem):
    gz, gy, gx = lax.axis_index("gz"), lax.axis_index("gy"), lax.axis_index("gx")
    other = 1 - gx

    def inside(dz, dy):
        z, y = gz + dz, gy + dy
        return (z >= 0) & (z < n_gz) & (y >= 0) & (y < n_gy)

    def dev(z, y, x):
        return {"gz": z, "gy": y, "gx": x}

    loads = [pltpu.make_async_copy(vol_hbm.at[:, z], vol.at[z], in_sem.at[z]) for z in range(4)]
    more = [
        pltpu.make_async_copy(a, b, in_sem.at[4 + i])
        for i, (a, b) in enumerate((
            (w1_hbm, wts.at[0]), (w2_hbm, wts.at[1]), (sidx_hbm, sidx), (seg_hbm, seg), (bm_hbm, bm)))
    ]
    for z in (0, 3, 1, 2):
        loads[z].start()
    for load in more:
        load.start()

    barrier = pltpu.get_barrier_semaphore()
    count = jnp.int32(1)
    pl.semaphore_signal(barrier, inc=1, device_id=dev(gz, gy, other), device_id_type=MESH)
    for dz, dy in SEAM:
        there = inside(dz, dy)
        count = count + there.astype(jnp.int32)

        @pl.when(there)
        def _():
            pl.semaphore_signal(barrier, inc=1, device_id=dev(gz + dz, gy + dy, gx), device_id_type=MESH)

    def pass_on(k):
        for sem, at, step in ((up_sem, k, 1), (down_sem, n_gz - 1 - k, -1)):
            @pl.when(gz == at)
            def _():
                if k > 0:
                    pl.semaphore_wait(sem, 1)
                if k < n_gz - 1:
                    pl.semaphore_signal(sem, inc=1, device_id=dev(gz + step, gy, gx), device_id_type=MESH)

    def rows_of(dy):
        if dy == 0:
            return slice(64, 320), slice(64, 320)
        return (slice(256, 320), slice(0, 64)) if dy == 1 else (slice(64, 128), slice(320, 384))

    def planes_of(kind, dz):
        if kind == "row":
            return slice(2, 6), slice(2, 6)
        if kind == "near":
            return (slice(5, 6), slice(1, 2)) if dz == 1 else (slice(2, 3), slice(6, 7))
        return (slice(4, 5), slice(0, 1)) if dz == 1 else (slice(3, 4), slice(7, 8))

    def halo_copy(d):
        kind, dz, dy = HALO[d]
        sr, dr = rows_of(dy)
        sp, dp = planes_of(kind, dz)
        return pltpu.make_async_remote_copy(
            src_ref=v.at[sp, sr, 256:512], dst_ref=v.at[dp, dr, 256:512], send_sem=send_sem.at[d], recv_sem=recv_sem.at[d],
            device_id=dev(gz + dz, gy + dy, gx), device_id_type=MESH)

    def mate_copy():
        return pltpu.make_async_remote_copy(
            src_ref=own_cols, dst_ref=mate_cols, send_sem=ms_sem, recv_sem=mr_sem,
            device_id=dev(gz, gy, other), device_id_type=MESH)

    def seam_copy(k):
        dz, dy = SEAM[k]
        part = (slice(0, 256), slice(128, 256), slice(0, 128))[dy]
        return pltpu.make_async_remote_copy(
            src_ref=seam.at[:, part], dst_ref=cols.at[1 - dy, 1 - dz, :, part], send_sem=ss_sem.at[k], recv_sem=sr_sem.at[k],
            device_id=dev(gz + dz, gy + dy, gx), device_id_type=MESH)

    def each(sign, act, *kinds):
        for d, (kind, dz, dy) in enumerate(HALO):
            if (kind if dy == 0 or dz == 0 else kind + "_corner") in kinds:
                @pl.when(inside(sign * dz, sign * dy))
                def _():
                    act(halo_copy(d))

    def each_seam(sign, act, first=0):
        for k, (dz, dy) in enumerate(SEAM):
            if k >= first:
                @pl.when(inside(sign * dz, sign * dy))
                def _():
                    act(seam_copy(k))

    def start(copy):
        copy.start()

    def wait_recv(copy):
        copy.wait_recv()

    def wait_send(copy):
        copy.wait_send()

    rr, cc = iota((256, 256), 0), iota((256, 256), 1)
    edge_lane = 255 * other
    side = 2 * other
    to_yc = one_hot(cc == (rr & 31) * 8 + (rr >> 5))

    def turn(z):
        loads[z].wait()
        v[z + 2, 64:320, 256:512] = mm(to_yc, vol[z].astype(F32).reshape(256, 256).astype(BF)).astype(BF)

    turn(0)
    turn(3)
    pl.semaphore_wait(barrier, count)
    pass_on(0)
    each(1, start, "near")
    turn(1)
    turn(2)
    each(1, start, "row")

    r16, l16 = iota((16, 256), 0), iota((16, 256), 1)
    lane = edge_lane + ((r16 >> 2) & 1) * (1 - 2 * other)
    packed = jnp.zeros((16, 256), F32)
    for z in range(4):
        mask = ((r16 & 3) == z) & (l16 == lane)
        packed = packed + mm_nt(one_hot(mask), v[z + 2, 64:320, 256:512])
    own_cols[...] = packed.astype(BF)
    mate_copy().start()
    each(1, start, "near_corner")
    pass_on(1)
    for load in more:
        load.wait()

    def build(r, band, edge):
        n_out = 6
        place = iota((32, 96), 1) - iota((32, 96), 0)
        wide = jnp.zeros((288, 96), F32)
        for b in range(3):
            wide = wide + mm(wts[r, :, b].reshape(288, 32), one_hot(place == 32 * b))
        wide = wide.astype(BF)
        tap, col = iota((96, 256 * n_out), 0), iota((96, 256 * n_out), 1)
        rows = mm(wide, one_hot(tap == (col & 255) - 32 * (col >> 8))).astype(BF)
        for y in range(n_out):
            for n in range(9):
                band[32 * y:32 * y + 32, 256 * n:256 * n + 256] = rows[32 * n:32 * n + 32, 256 * y:256 * y + 256]
                if y < 2:
                    edge[32 * y:32 * y + 32, 128 * n:128 * n + 128] = rows[32 * n:32 * n + 32, 256 * y:256 * y + 128]

    build(0, band1, band1e)
    mate_copy().wait_recv()
    both = jnp.where(r16 < 8, own_cols[...].astype(F32), mate_cols[...].astype(F32)).astype(BF)
    seam[...] = both
    each_seam(1, start)
    each(1, start, "far")
    each(1, start, "far_corner")
    for kind, dz, dy in HALO:
        @pl.when(jnp.logical_not(inside(-dz, -dy)))
        def _():
            rows, planes = rows_of(dy)[1], planes_of(kind, dz)[1]
            v[planes, rows, 256:512] = jnp.zeros((planes.stop - planes.start, rows.stop - rows.start, 256), BF)
    for dz, dy in SEAM:
        @pl.when(jnp.logical_not(inside(-dz, -dy)))
        def _():
            cols[1 - dy, 1 - dz] = jnp.zeros((16, 256), BF)
    cols[1, 1] = both
    def product(bands, ref, p, lo, hi, piece):
        edge, first, _ = piece
        n = WIDTH[edge]
        rhs = [ref[p + i, first:first + n, 256 * c:256 * c + 256] for i in range(lo, hi) for c in range(3)]
        return mm(bands[edge][:, 3 * n * lo:3 * n * hi], jnp.concatenate(rhs, axis=0))

    def rows_out(piece):
        return slice(piece[2], piece[2] + DEPTH[piece[0]])

    def widened(x, col):
        lanes = iota(x.shape, 1)
        left = jnp.where(lanes == 0, jnp.where(gx == 1, col, 0.0), pltpu.roll(x, 1, 1))
        right = jnp.where(lanes == 255, jnp.where(gx == 0, col, 0.0), pltpu.roll(x, 255, 1))
        return left.astype(BF), right.astype(BF)

    def widen(p, first, last):
        at = slice(first, last)
        x = v[p, at, 256:512].astype(F32)
        v[p, at, 0:256], v[p, at, 512:768] = widened(x, t[at, 8 + p:9 + p])

    def valid(shape, q, first):
        row = iota(shape, 0) + first
        ok = ((row >= 32) | (gy > 0)) & ((row < 288) | (gy < n_gy - 1))
        return ok & ((q > 0) | (gz > 0)) & ((q < 5) | (gz < n_gz - 1))

    def hide(q, piece, x, seamed):
        at = rows_out(piece)
        x = jnp.where(valid(x.shape, q, at.start), jnp.maximum(x, 0.0), 0.0)
        h[q, at, 256:512] = x.astype(BF)
        h[q, at, 0:256], h[q, at, 512:768] = widened(x, hs[at, q:q + 1] if seamed else 0.0)

    def insert_seam(q):
        lanes = iota((320, 128), 1)
        for x, lane, at in ((0, 127, slice(640, 768)), (1, 0, slice(0, 128))):
            old = h[q, 0:320, at].astype(F32)
            h[q, 0:320, at] = jnp.where((lanes == lane) & (gx == x), hs[:, q:q + 1], old).astype(BF)

    row, col = iota((48, 128), 0), iota((48, 128), 1)
    core = (row >> 3) & 1
    j = (row >> 2) & 1
    plane = (row & 3) + 4 * (row >> 4) - 2
    tap = jnp.where(core == 0, 2 - side, jnp.where(j == 0, 1, side))
    put = one_hot((j + (1 - core) < 2) & (plane >= 0) & (plane < 8) & (col == 8 * tap + plane))

    def unpack(dy, picked, n):
        to, part, rows = (
            (slice(0, 64), slice(128, 256), slice(64, 128)),
            (slice(64, 320), slice(0, 256), slice(0, 256)),
            (slice(320, 384), slice(0, 128), slice(0, 64)))[dy]
        packed = cols[dy, picked, :, part]
        placed = mm_tn(packed.reshape(16 * n, part.stop - part.start), put[16 * picked.start:16 * picked.stop])
        t[to, :] = placed[rows]

    def seams():
        every = t[...]
        moved = [every if n == 0 else pltpu.roll(every, 128 - n, 1) for n in (8 * c + a for a in range(3) for c in range(3))]
        for piece in PIECES1:
            edge, first, out = piece
            n = DEPTH[edge]
            z = jnp.concatenate([m[first:first + WIDTH[edge]].astype(BF) for m in moved], axis=0)
            x = mm(bands1[edge][...], z)
            row, lanes = iota((n, 128), 0) + out, iota((n, 128), 1)
            ok = ((row >= 32) | (gy > 0)) & ((row < 288) | (gy < n_gy - 1))
            ok = ok & ((lanes > 0) | (gz > 0)) & ((lanes < 5) | (gz < n_gz - 1))
            hs[out:out + n] = jnp.where(ok, jnp.maximum(x, 0.0), 0.0)

    s = sidx[...]
    s_x, s_y, s_z = s & 255, (s >> 8) & 7, s >> 11
    select_x = one_hot(rr == s_x)
    to_cy = one_hot(cc == (rr & 7) * 32 + (rr >> 3))
    acc[...] = jnp.zeros((256, 256), F32)

    def finish(z, piece, x):
        at = rows_out(piece)
        made[z, at] = (x + v[z + 2, 64 + at.start:64 + at.stop, 256:512].astype(F32)).astype(BF)

    def pick(z):
        acc[...] = jnp.where(s_z == z, mm(made[z], select_x), acc[...])

    def put_out(z):
        feat[:, z] = mm(to_cy, made[z]).reshape(32, 8, 256).astype(BF)

    bands1, bands2 = (band1, band1e), (band2, band2e)
    middle, edges = PIECES1[0], PIECES1[1:]

    unpack(1, slice(1, 2), 1)
    for p in range(2, 6):
        widen(p, 64, 320)
    for q in (2, 3):
        hide(q, middle, product(bands1, v, q, 0, 3, middle), False)
    for q, lo, hi in ((1, 1, 3), (4, 0, 2), (0, 2, 3), (5, 0, 1)):
        part1[q, rows_out(middle)] = product(bands1, v, q, lo, hi, middle)
    for k in range(2, min(3, n_gz)):
        pass_on(k)
    build(1, band2, band2e)
    for k in range(3, n_gz):
        pass_on(k)

    label = iota((NSEG, 256), 0)
    own_seg = one_hot(label == seg[gz])
    for off in range(n_gz):
        block = lax.rem(gz + n_gz - off, n_gz)
        same[off] = mm_tn(one_hot(label == seg[block]), own_seg)

    each(-1, wait_recv, "row")
    for k in (0, 1):
        @pl.when(inside(*(-d for d in SEAM[k])))
        def _():
            seam_copy(k).wait_recv()
    for dy in (0, 2):
        unpack(dy, slice(1, 2), 1)
    for p in range(2, 6):
        widen(p, 0, 64)
        widen(p, 320, 384)
    for q in (2, 3):
        for piece in edges:
            hide(q, piece, product(bands1, v, q, 0, 3, piece), False)
    for q, lo, hi in ((1, 1, 3), (4, 0, 2), (0, 2, 3), (5, 0, 1)):
        for piece in edges:
            part1[q, rows_out(piece)] = product(bands1, v, q, lo, hi, piece)

    each(-1, wait_recv, "near", "near_corner")
    each_seam(-1, wait_recv, 2)
    for dy in range(3):
        unpack(dy, slice(0, 3), 3)
    for p in (1, 6):
        widen(p, 0, 384)
    for q, lo in ((1, 0), (4, 2)):
        for piece in PIECES1:
            hide(q, piece, part1[q, rows_out(piece)] + product(bands1, v, q, lo, lo + 1, piece), False)
    seams()
    for q in range(1, 5):
        insert_seam(q)
    for q in (0, 5):
        for piece in PIECES1:
            at = rows_out(piece)
            part1[q, at] = part1[q, at] + product(bands1, v, q, 1, 2, piece)
    for z in (1, 2):
        for piece in PIECES2:
            finish(z, piece, product(bands2, h, z, 0, 3, piece))
    for i, z, lo in ((0, 0, 1), (1, 3, 0)):
        for piece in PIECES2:
            part2[i, rows_out(piece)] = product(bands2, h, z, lo, lo + 2, piece)
    for z in (1, 2):
        pick(z)
        put_out(z)

    each(-1, wait_recv, "far", "far_corner")
    for p in (0, 7):
        widen(p, 0, 384)
    for q, lo in ((0, 0), (5, 2)):
        for piece in PIECES1:
            hide(q, piece, part1[q, rows_out(piece)] + product(bands1, v, q, lo, lo + 1, piece), True)
    for i, z, lo in ((0, 0, 0), (1, 3, 2)):
        for piece in PIECES2:
            finish(z, piece, part2[i, rows_out(piece)] + product(bands2, h, z, lo, lo + 1, piece))
    pick(0)
    pick(3)

    picked = jnp.where((rr >> 5) == s_y, acc[...], 0.0)
    picked = jnp.sum(picked.reshape(8, 32, 256), axis=0)
    norm = jnp.sqrt(jnp.sum(picked * picked, axis=0, keepdims=True) + 1.0)
    emb_all[0] = (picked / norm).astype(BF)

    def emb_copy(off):
        return pltpu.make_async_remote_copy(
            src_ref=emb_all.at[0], dst_ref=emb_all.at[off], send_sem=es_sem.at[off], recv_sem=er_sem.at[off],
            device_id=dev(lax.rem(gz + off, n_gz), gy, gx), device_id_type=MESH)

    for k in range(1, n_gz):
        emb_copy(jnp.where(2 * gz < n_gz, n_gz - k, k)).start()
    put_out(0)
    put_out(3)

    own = emb_all[0]
    total = jnp.zeros((1, 256), F32)
    positive = jnp.zeros((1, 256), F32)
    for k in range(n_gz):
        off = jnp.where(2 * gz < n_gz, n_gz - k, k) if k else 0
        block = lax.rem(gz + n_gz - off, n_gz)
        if k:
            emb_copy(off).wait_recv()
        e = jnp.exp(mm_tn(emb_all[off], own) * 4.0) * bm[gz, block].astype(F32)
        total = total + jnp.sum(e, axis=0, keepdims=True)
        positive = positive + jnp.sum(e * same[off], axis=0, keepdims=True)
    loss[...] = jnp.log(total) - jnp.log(positive)
    for off in range(1, n_gz):
        emb_copy(off).wait_send()
    each(1, wait_send, "near", "row", "near_corner", "far", "far_corner")
    each_seam(1, wait_send)
    mate_copy().wait_send()


def write_out(feat, loss, feat_hbm, loss_hbm, sem):
    copies = [pltpu.make_async_copy(feat, feat_hbm, sem.at[0]), pltpu.make_async_copy(loss, loss_hbm, sem.at[1])]
    for copy in copies:
        copy.start()
    for copy in copies:
        copy.wait()


def shards(n_gz, n_gy, volume, first_weight, second_weight, sample_index, segments, block_match):
    vmem = pl.BlockSpec(memory_space=pltpu.VMEM)
    dma = pltpu.SemaphoreType.DMA
    features, row_loss = pl.pallas_call(
        functools.partial(kernel, n_gz, n_gy),
        out_shape=(
            jax.ShapeDtypeStruct(volume.shape, BF),
            jax.ShapeDtypeStruct((1, 256), F32),
        ),
        in_specs=[pl.BlockSpec(memory_space=pltpu.MemorySpace.HBM)] * 6,
        out_specs=(vmem, vmem),
        scratch_shapes=[
            pltpu.VMEM((4, 32, 8, 256), BF),
            pltpu.VMEM((2, 3, 3, 3, 32, 32), BF),
            pltpu.VMEM((1, 256), jnp.int32),
            pltpu.VMEM((n_gz, 1, 256), jnp.int32),
            pltpu.SMEM(block_match.shape, jnp.int32),
            pltpu.VMEM((8, 384, 768), BF),
            pltpu.VMEM((6, 320, 768), BF),
            pltpu.VMEM((192, 2304), BF),
            pltpu.VMEM((64, 1152), BF),
            pltpu.VMEM((192, 2304), BF),
            pltpu.VMEM((64, 1152), BF),
            pltpu.VMEM((6, 320, 256), F32),
            pltpu.VMEM((2, 256, 256), F32),
            pltpu.VMEM((16, 256), BF),
            pltpu.VMEM((16, 256), BF),
            pltpu.VMEM((16, 256), BF),
            pltpu.VMEM((3, 3, 16, 256), BF),
            pltpu.VMEM((384, 128), F32),
            pltpu.VMEM((320, 128), F32),
            pltpu.VMEM((4, 256, 256), BF),
            pltpu.VMEM((n_gz, 256, 256), F32),
            pltpu.VMEM((n_gz, 32, 256), BF),
            pltpu.VMEM((256, 256), F32),
            dma((9,)), dma((len(HALO),)), dma((len(HALO),)), dma, dma, dma((len(SEAM),)), dma((len(SEAM),)), dma((n_gz,)), dma((n_gz,)),
            pltpu.SemaphoreType.REGULAR, pltpu.SemaphoreType.REGULAR,
        ],
        compiler_params=pltpu.CompilerParams(
            collective_id=0, has_side_effects=True, vmem_limit_bytes=40 << 20),
        name="voxel_contrast",
    )(
        *(pltpu.with_memory_space_constraint(a, pltpu.MemorySpace.HBM) for a in (
            volume, first_weight, second_weight, sample_index.reshape(1, 256),
            segments.reshape(segments.shape[0], 1, 256), block_match)),
    )
    hbm = pl.BlockSpec(memory_space=pltpu.MemorySpace.HBM)
    features, row_loss = pl.pallas_call(
        write_out,
        out_shape=(jax.ShapeDtypeStruct(volume.shape, BF), jax.ShapeDtypeStruct((1, 256), F32)),
        in_specs=[vmem, vmem],
        out_specs=(hbm, hbm),
        scratch_shapes=[dma((2,))],
        name="write_out",
    )(*(pltpu.with_memory_space_constraint(a, pltpu.MemorySpace.VMEM) for a in (features, row_loss)))
    return features, row_loss.reshape(1, 1, 1, 256)


def solution(mesh):
    in_specs = (
        P(None, ("group", "gz"), "gy", "gx"),
        P(),
        P(),
        P(("group", "gz"), "gy", "gx", None),
        P("group", "gy", "gx", None),
        P("group", None),
    )
    out_specs = (P(None, ("group", "gz"), "gy", "gx"), P(("group", "gz"), "gy", "gx", None))
    body = functools.partial(shards, mesh.shape["gz"], mesh.shape["gy"])
    return jax.shard_map(body, mesh=mesh, in_specs=in_specs, out_specs=out_specs, check_vma=False)
```
